32 devices in a mesh: freq: 2 (over y), cells: 16 (over z, x, core).
Axes of the slice: x: 2, y: 2, z: 4, core: 2. Of those that a mesh axis runs over, the one named last changes fastest.
Arguments:
- jacobian_tiles: bfloat16 [8, 48, 20, 128, 128], P('freq', 'cells'), may hold values from -0.29882812 to 0.29882812
- tip_lists: int32 [48, 20], P('cells'), may hold values from 0 to 31, as said below
- counts: int32 [48], P('cells'), may hold values from 1 to 20, as said below
- residual: bfloat16 [8, 4096], P('freq'), may hold values from -6 to 6
Outputs:
- normal_band: float32 [48, 5, 3, 128, 128], P('cells', None, None, 'freq')
- gradient: float32 [6144], P('cells')
The draws below stay inside these ranges and needn't reach their ends.
Inputs may be any that keep to these rules, and one draw needn't show every extreme that they name: `tip_lists`: each cell block's list names 20 different tip blocks, consecutive modulo 32. The first counts[a] slots of cell block a are live.
All inputs are finite; a program needn't handle non-finite values.
Results may differ from the reference program's by a relative error of at most 0.0003.
Values may be sent and summed in bfloat16 or wider, within the bound.
No kernel may reach another device: no remote copies, remote signals or barrier semaphores. Data moves between devices by JAX's collectives and lax.ppermute only.
A program may use at most 192 MiB of HBM per device.

```python
import jax
import jax.numpy as jnp
from jax import lax

TILE = 128
TIPB = 32
FREQS = 8
FOOT = 20
SHIFTS = 4
CB_DEV = 3
NCB = 48
NCELLS = 6144
TIPS = 4096
N_CELLS = 16


def draw_tip_lists(key, part):
    jitter = jax.random.randint(jax.random.fold_in(key, 11), (NCB,), -2, 3, dtype=jnp.int32)
    starts = jnp.arange(NCB, dtype=jnp.int32) * TIPB // NCB + jitter
    lists = (starts[:, None] + jnp.arange(FOOT, dtype=jnp.int32)[None, :]) % TIPB
    return lists.astype(jnp.int32)


def draw_counts(key, part):
    values = jax.random.randint(jax.random.fold_in(key, 21), (NCB,), 1, FOOT + 1, dtype=jnp.int32)
    first_pick = jax.random.randint(jax.random.fold_in(key, 22), (), 0, NCB, dtype=jnp.int32)
    step_pick = jax.random.randint(jax.random.fold_in(key, 23), (), 0, NCB - 1, dtype=jnp.int32)
    second_pick = (first_pick + 1 + step_pick) % NCB
    values = values.at[first_pick].set(FOOT)
    values = values.at[second_pick].set(1)
    return values.astype(jnp.int32)


def steps_of(rng, shape, shards, low, largest):
    def one(dim, parts):
        draws = jax.random.uniform(jax.random.fold_in(jax.random.fold_in(rng, 6), dim), (parts,), jnp.float32, low / len(shards), largest / len(shards))
        return jnp.repeat(jnp.exp(draws), shape[dim] // parts).reshape((-1,) + (1,) * (len(shape) - dim - 1))

    loudness = one(*shards[0])
    for cut in shards[1:]:
        loudness = loudness * one(*cut)
    return loudness


def gaussian(stream_key, shape, scale, limit, split=(), held_as=jnp.bfloat16):
    array = jax.random.normal(stream_key, shape, jnp.float32) * scale
    if len(split) > 0:
        array = steps_of(stream_key, shape, split, -0.22, 0.18) * array
    return jnp.clip(array, min=-limit, max=limit).astype(held_as)


def setup_inputs(seed: int = 0) -> dict:
    seeds = jax.random.split(jax.random.key(seed), 5)
    return {
        "jacobian_tiles": gaussian(seeds[0], (FREQS, NCB, FOOT, TILE, TILE), 0.05, 0.29882812, ((0, 2), (1, 16))),
        "tip_lists": draw_tip_lists(jax.random.fold_in(seeds[4], 71), 0),
        "counts": draw_counts(jax.random.fold_in(seeds[4], 71), 0),
        "residual": gaussian(seeds[3], (FREQS, TIPS), 1.0, 6.0, ((0, 2),)),
    }


def panel_products(local_tiles, local_tips, local_live, far_tiles, far_tips, far_live):
    matches = (local_tips[:, :, None, None] == far_tips[None, None, :, :]).astype(jnp.float32)
    matches = matches * local_live[:, :, None, None] * far_live[None, None, :, :]
    matched = jnp.einsum('apbq,fbqik->fabpik', matches, far_tiles, precision=lax.Precision.HIGHEST)
    return jnp.einsum('fapij,fabpik->abjk', local_tiles, matched, precision=lax.Precision.HIGHEST)


def reference(jacobian_tiles, tip_lists, counts, residual):
    slot_ids = jnp.arange(FOOT, dtype=jnp.int32)
    live_mask = (slot_ids[None, :] < counts[:, None]).astype(jnp.float32)
    tip_ids = jnp.arange(TIPB, dtype=jnp.int32)
    resid_blocks = residual.astype(jnp.float32).reshape(FREQS, TIPB, TILE)

    def one_device(device):
        first = (device * CB_DEV).astype(jnp.int32)
        local_tiles = lax.dynamic_slice_in_dim(jacobian_tiles, first, CB_DEV, 1).astype(jnp.float32)
        local_tips = lax.dynamic_slice_in_dim(tip_lists, first, CB_DEV, 0)
        local_live = lax.dynamic_slice_in_dim(live_mask, first, CB_DEV, 0)
        blocks = []
        for offset in range(SHIFTS + 1):
            far_first = (((device + offset) % N_CELLS) * CB_DEV).astype(jnp.int32)
            far_tiles = lax.dynamic_slice_in_dim(jacobian_tiles, far_first, CB_DEV, 1).astype(jnp.float32)
            far_tips = lax.dynamic_slice_in_dim(tip_lists, far_first, CB_DEV, 0)
            far_live = lax.dynamic_slice_in_dim(live_mask, far_first, CB_DEV, 0)
            blocks.append(panel_products(local_tiles, local_tips, local_live, far_tiles, far_tips, far_live))
        onehot = (local_tips[:, :, None] == tip_ids[None, None, :]).astype(jnp.float32) * local_live[:, :, None]
        picked = jnp.einsum('apt,fti->fapi', onehot, resid_blocks, precision=lax.Precision.HIGHEST)
        grad_part = jnp.einsum('fapij,fapi->aj', local_tiles, picked, precision=lax.Precision.HIGHEST)
        return jnp.stack(blocks, axis=1), grad_part.reshape(CB_DEV * TILE)

    bands, grads = lax.map(one_device, jnp.arange(N_CELLS, dtype=jnp.int32))
    normal_band = bands.reshape(NCB, SHIFTS + 1, CB_DEV, TILE, TILE)
    gradient = grads.reshape(NCELLS)
    return normal_band, gradient
```

```python
import functools

import jax
import jax.numpy as jnp
from jax import lax
from jax.experimental import pallas as pl
from jax.experimental.pallas import tpu as pltpu
from jax.sharding import PartitionSpec as P

SHIFTS = 4
GROUP = 2
ROW = 4

LEVELS = (32, 36, 40, 44, 50)
CUTS = (12, 22, 30, 36)

SMEM = pl.BlockSpec(memory_space=pltpu.SMEM)
VMEM = pl.BlockSpec(memory_space=pltpu.VMEM)
ANY = pl.BlockSpec(memory_space=pl.ANY)


def popcount(x):
    srl = lax.shift_right_logical
    x = x - (srl(x, jnp.int32(1)) & 0x55555555)
    x = (x & 0x33333333) + (srl(x, jnp.int32(2)) & 0x33333333)
    x = (x + srl(x, jnp.int32(4))) & 0x0F0F0F0F
    x = x + srl(x, jnp.int32(8))
    x = x + srl(x, jnp.int32(16))
    return x & 63


def list_kernel(n, nb, slots, tips, where, meta, zsend, xsend, acode, bcode, nums, live, union):
    srl = lax.shift_right_logical
    l, xcol = where[0], where[1]

    def fill(dev, _):
        total = jnp.int32(0)
        for b in range(nb):
            j = dev * nb + b
            start, count = meta[2 * j], meta[2 * j + 1]
            ones = (jnp.int32(1) << count) - 1
            bits = (ones << start) | srl(srl(ones, tips - 1 - start), jnp.int32(1))
            if tips < 32:
                bits = bits & ((1 << tips) - 1)
            live[j] = bits
            total = total | bits
        union[dev] = total
        return 0

    lax.fori_loop(0, n, fill, 0)

    def wrap(dev):
        return lax.rem(dev + n, n)

    def z_target(dev):
        base = (dev // ROW) * ROW
        at = dev - base
        total = union[wrap(base - 1)]
        for back in range(2, ROW + 1):
            got = union[wrap(base - back)]
            total = total | jnp.where(ROW - back >= at, got, 0)
        return total

    def x_target(dev):
        base = (dev // ROW) * ROW
        return union[base] | union[base + 1]

    def chip_counts(chip, most):
        zsum, xsum = jnp.int32(0), jnp.int32(0)
        for core in range(2):
            dev = 2 * chip + core
            zt, xt = z_target(dev), x_target(dev)
            for b in range(nb):
                bits = live[dev * nb + b]
                zsum = zsum + popcount(bits & zt)
                xsum = xsum + popcount(bits & xt)
        xsum = jnp.where(lax.rem(chip, 2) == 1, xsum, 0)
        return jnp.maximum(most, jnp.maximum(zsum, xsum))

    nums[4] = lax.fori_loop(0, n // 2, chip_counts, jnp.int32(0))

    own = union[l]

    def build(first, z, out, coded):
        def panel(jj, at):
            dev = first + jj // nb
            b = lax.rem(jj, nb)
            j = dev * nb + b
            target = jnp.where(z, z_target(dev), x_target(dev))
            need = live[j] & target
            start = meta[2 * j]
            shift = dev - l

            def slot(p, at):
                tip = start + p
                tip = jnp.where(tip >= tips, tip - tips, tip)
                if coded:
                    code = (shift * nb + b) * tips + tip
                    good = (shift >= 0) & (shift <= SHIFTS) & ((srl(own, tip) & 1) == 1)
                    out[at] = jnp.where(good, code, -1)
                else:
                    out[at] = jj * slots + p
                return at + (srl(need, tip) & 1)

            return lax.fori_loop(0, meta[2 * j + 1], slot, at)

        return lax.fori_loop(0, 2 * nb, panel, jnp.int32(0))

    mine = 2 * xcol
    nums[0] = build(mine, True, zsend, False)
    nums[1] = build(mine, False, xsend, False)
    nums[2] = build(ROW + mine, True, acode, True)
    nums[3] = build(jnp.where(xcol == 0, 2, ROW), xcol == 1, bcode, True)


def pack_kernel(half, nb, slots, where, zsend, xsend, nums, own, peer, zout, xout, sems):
    core = where[2]

    def issue(which, todo, listed, out, count):
        def one(s, _):
            e = listed[2 * s + core]
            jj = e // slots
            p = lax.rem(e, slots)
            b = lax.rem(jj, nb)
            mine = (jj // nb) == core
            for source, yes in ((own, mine), (peer, jnp.logical_not(mine))):

                @pl.when(yes)
                def _():
                    copy = pltpu.make_async_copy(
                        source.at[:, b, p], out.at[s], sems.at[which, s]
                    )
                    copy.start() if todo else copy.wait()

            return 0

        lax.fori_loop(0, jnp.clip((count - core + 1) // 2, 0, half), one, 0)

    for todo in (True, False):
        issue(0, todo, zsend, zout, nums[0])
        issue(1, todo, xsend, xout, jnp.where(where[1] == 1, nums[1], 0))


def product(left, tile):
    flat = tile.reshape(tile.shape[0] * tile.shape[1], tile.shape[2])
    return jnp.dot(left, flat, preferred_element_type=jnp.float32)


def add_to(acc, kb, got):
    nf, nb, _, rows, _ = acc.shape
    for a in range(nb):
        for h in range(nf):
            at = (a * nf + h) * rows
            acc[h, a, kb] += got[at : at + rows]


def run_list(count, group, entry, left, acc):
    def some(i, _):
        found = [entry(group * i + g) for g in range(group)]
        got = [product(left[t], tile) for t, tile, _ in found]
        for (_, _, kb), part in zip(found, got):
            add_to(acc, kb, part)
        return 0

    lax.fori_loop(0, (count + group - 1) // group, some, 0)


def own_kernel(nb, tips, meta, raw, resid, left, acc, grad):
    freqs, width = raw.shape[0], raw.shape[-1]
    acc[...] = jnp.zeros_like(acc)
    grad[...] = jnp.zeros_like(grad)

    def turn(t, _):
        for a in range(nb):
            start, count = meta[2 * a], meta[2 * a + 1]
            p = t - start
            p = jnp.where(p < 0, p + tips, p)

            @pl.when(p < count)
            def _():
                for f in range(freqs):
                    left[t, pl.ds(a * width, width), pl.ds(f * width, width)] = raw[f, a, p].T

            @pl.when(p >= count)
            def _():
                left[t, pl.ds(a * width, width), :] = jnp.zeros(
                    (width, freqs * width), left.dtype
                )

        return 0

    lax.fori_loop(0, tips, turn, 0)

    left[tips] = jnp.zeros(left.shape[1:], left.dtype)
    for b in range(nb):
        start, count = meta[2 * b], meta[2 * b + 1]

        def one(i, _):
            for g in range(GROUP):
                p = GROUP * i + g
                t = start + p
                t = jnp.where(t >= tips, t - tips, t)
                t = jnp.where(p < count, t, tips)
                tile = raw[:, b, jnp.minimum(p, count - 1)]
                add_to(acc, b, product(left[t], tile))
                grad[b] += product(resid[t], tile)
            return 0

        lax.fori_loop(0, (count + GROUP - 1) // GROUP, one, 0)


def peer_kernel(tips, where, meta, left, raw, acc_in, acc):
    acc[...] = acc_in[...]
    nb = raw.shape[1]

    @pl.when(where[2] == 0)
    def _():
        for b in range(nb):
            j = nb + b
            start, count = meta[2 * j], meta[2 * j + 1]

            def entry(p):
                t = start + p
                t = jnp.where(t >= tips, t - tips, t)
                t = jnp.where(p < count, t, tips)
                return t, raw[:, b, jnp.minimum(p, count - 1)], nb + b

            run_list(count, GROUP, entry, left, acc)


def chunk_kernel(tips, spans, where, acode, bcode, nums, left, acc_in, *rest):
    arrays, acc = rest[:-1], rest[-1]
    acc[...] = acc_in[...]
    core = where[2]
    for (second, other, offset), tiles in zip(spans, arrays):
        codes = bcode if second else acode
        count = nums[3] if second else nums[2]
        holder = 1 - core if other else core
        held = jnp.clip((count - holder + 1) // 2 - offset, 0, tiles.shape[0])

        def entry(s):
            at = jnp.minimum(s, held - 1)
            code = codes[2 * (at + offset) + holder]
            good = (code >= 0) & (s < held)
            t = jnp.where(good, lax.rem(code, tips), tips)
            return t, tiles[at], jnp.where(good, code // tips, acc.shape[2] - 1)

        run_list(held, GROUP, entry, left, acc)


def call(kernel, outs, specs, out_specs, scratch=(), name=None, cost_us=0):
    return pl.pallas_call(
        kernel,
        out_shape=outs,
        in_specs=specs,
        out_specs=out_specs,
        scratch_shapes=scratch,
        name=name,
        cost_estimate=pl.CostEstimate(
            flops=int(cost_us * 1e9), transcendentals=0, bytes_accessed=int(cost_us * 1e6)
        ),
        compiler_params=pltpu.CompilerParams(vmem_limit_bytes=60000 * 1024),
    )


def on_device(tiles, tip_lists, counts, residual):
    freqs, nb, slots, width = tiles.shape[:4]
    tips = residual.shape[1] // width
    n = lax.axis_size("cells")
    nf = lax.axis_size("freq")
    rows = width // nf
    d = lax.axis_index("cells").astype(jnp.int32)
    fi = lax.axis_index("freq")
    i32 = jnp.int32

    def moved(x, to):
        return lax.ppermute(x, "cells", [(i, to(i) % n) for i in range(n)])

    peer = moved(tiles, lambda i: i ^ 1)

    own_meta = jnp.stack([tip_lists[:, 0], counts], axis=1).reshape(-1).astype(i32)
    meta = own_meta
    have = 1
    while have < n:
        more = moved(meta, lambda i: i - have)
        take = min(have, n - have) * 2 * nb
        meta = jnp.concatenate([meta, more[:take]])
        have = min(2 * have, n)
    l = lax.rem(d, i32(ROW))
    xcol = lax.rem(d // 2, i32(2))
    core = lax.rem(d, i32(2))
    where = jnp.stack([l, xcol, core])
    per = 2 * nb
    row_meta = lax.dynamic_slice(
        jnp.concatenate([meta, meta]), (lax.rem(n - l, i32(n)) * per,), (n * per,)
    )

    ints = lambda m: jax.ShapeDtypeStruct((m,), i32)
    most = 2 * nb * slots
    zsend, xsend, acode, bcode, nums = call(
        functools.partial(list_kernel, n, nb, slots, tips),
        (ints(most + 8), ints(most + 8), ints(most + 8), ints(most + 8), ints(8)),
        [SMEM] * 2,
        (SMEM,) * 5,
        [pltpu.SMEM((n * nb,), i32), pltpu.SMEM((n,), i32)],
        name="lists",
        cost_us=6,
    )(where, row_meta)

    resid = residual.reshape(freqs, tips, width).transpose(1, 0, 2).reshape(tips, 1, freqs * width)
    resid = jnp.pad(jnp.broadcast_to(resid, (tips, 16, freqs * width)), ((0, 1), (0, 0), (0, 0)))
    acc_shape = jax.ShapeDtypeStruct((nf, nb, (SHIFTS + 1) * nb + 1, rows, width), jnp.float32)
    left, acc, grad = call(
        functools.partial(own_kernel, nb, tips),
        (
            jax.ShapeDtypeStruct((tips + 1, nb * width, freqs * width), tiles.dtype),
            acc_shape,
            jax.ShapeDtypeStruct((nb, 16, width), jnp.float32),
        ),
        [SMEM, VMEM, VMEM],
        (VMEM, VMEM, VMEM),
        name="own",
        cost_us=25,
    )(own_meta, tiles, resid)
    acc = call(
        functools.partial(peer_kernel, tips),
        acc_shape,
        [SMEM, SMEM, VMEM, VMEM, VMEM],
        VMEM,
        name="peer",
        cost_us=12,
    )(where, meta, left, peer, acc)

    def main(cuts):
        half = cuts[-1]
        packed = jax.ShapeDtypeStruct((half, freqs, width, width), tiles.dtype)
        zpack, xpack = call(
            functools.partial(pack_kernel, half, nb, slots),
            (packed, packed),
            [SMEM] * 4 + [ANY] * 2,
            (VMEM, VMEM),
            [pltpu.SemaphoreType.DMA((2, half))],
            name="pack",
            cost_us=6,
        )(where, zsend, xsend, nums, tiles, peer)
        total = acc
        waiting = []
        for at, end in zip((0,) + cuts, cuts):
            a = moved(zpack[at:end], lambda i: i - ROW)
            a_peer = moved(a, lambda i: i ^ 1)
            b = moved(jnp.where(xcol == 0, a, xpack[at:end]), lambda i: i ^ 2)
            b_peer = moved(b, lambda i: i ^ 1)
            now = waiting + [((False, False, at), a), ((False, True, at), a_peer)]
            waiting = [((True, False, at), b), ((True, True, at), b_peer)]
            for some in (now, waiting) if end == half else (now,):
                total = call(
                    functools.partial(chunk_kernel, tips, [s for s, _ in some]),
                    acc_shape,
                    [SMEM] * 4 + [VMEM] * (2 + len(some)),
                    VMEM,
                    name="chunk",
                    cost_us=12,
                )(where, acode, bcode, nums, left, total, *[x for _, x in some])
        return total

    full = nb * slots
    levels = [full * m // 60 for m in LEVELS] + [full]
    need = (nums[4] + 1) // 2
    level = sum((need > h).astype(i32) for h in levels[:-1])

    def cuts_of(half):
        return tuple(half * m // 36 for m in CUTS)

    total = lax.switch(level, [functools.partial(main, cuts_of(h)) for h in levels])
    total = total[:, :, :-1]

    band = lax.dynamic_index_in_dim(total, fi, 0, keepdims=False)
    grad = grad[:, 0, :]
    grad_sum = grad
    for s in range(1, nf):
        pairs = [(i, (i + s) % nf) for i in range(nf)]
        part = lax.dynamic_index_in_dim(total, lax.rem(fi + s, nf), 0, keepdims=False)
        band = band + lax.ppermute(part, "freq", pairs)
        grad_sum = grad_sum + lax.ppermute(grad, "freq", pairs)
    return (
        band.reshape(nb, SHIFTS + 1, nb, rows, width),
        grad_sum.reshape(nb * width),
    )


def solution(mesh):
    placed = (P("freq", "cells", None, None, None), P("cells", None), P("cells"), P("freq", None))
    return jax.shard_map(
        on_device,
        mesh=mesh,
        in_specs=placed,
        out_specs=(P("cells", None, None, "freq", None), P("cells")),
        check_vma=False,
    )
```

```python
import functools

import jax
import jax.numpy as jnp
from jax import lax
from jax.experimental import pallas as pl
from jax.experimental.pallas import tpu as pltpu
from jax.sharding import PartitionSpec as P

SHIFTS = 4
GROUP = 2
ROW = 4

LEVELS = (31, 34, 37, 40, 43, 48)
CUTS = (6, 13, 21, 29, 36)

SMEM = pl.BlockSpec(memory_space=pltpu.SMEM)
VMEM = pl.BlockSpec(memory_space=pltpu.VMEM)
ANY = pl.BlockSpec(memory_space=pl.ANY)


def popcount(x):
    srl = lax.shift_right_logical
    x = x - (srl(x, jnp.int32(1)) & 0x55555555)
    x = (x & 0x33333333) + (srl(x, jnp.int32(2)) & 0x33333333)
    x = (x + srl(x, jnp.int32(4))) & 0x0F0F0F0F
    x = x + srl(x, jnp.int32(8))
    x = x + srl(x, jnp.int32(16))
    return x & 63


def list_kernel(n, nb, slots, tips, where, meta, zsend, xsend, codes, nums, live, union):
    srl = lax.shift_right_logical
    l, xcol = where[0], where[1]

    def fill(dev, _):
        total = jnp.int32(0)
        for b in range(nb):
            j = dev * nb + b
            start, count = meta[2 * j], meta[2 * j + 1]
            ones = (jnp.int32(1) << count) - 1
            bits = (ones << start) | srl(srl(ones, tips - 1 - start), jnp.int32(1))
            if tips < 32:
                bits = bits & ((1 << tips) - 1)
            live[j] = bits
            total = total | bits
        union[dev] = total
        return 0

    lax.fori_loop(0, n, fill, 0)

    def wrap(dev):
        return lax.rem(dev + n, n)

    def z_target(dev):
        base = (dev // ROW) * ROW
        at = dev - base
        total = union[wrap(base - 1)]
        for back in range(2, ROW + 1):
            got = union[wrap(base - back)]
            total = total | jnp.where(ROW - back >= at, got, 0)
        return total

    def x_target(dev):
        base = (dev // ROW) * ROW
        return union[base] | union[base + 1]

    def chip_counts(chip, most):
        zsum, xsum = jnp.int32(0), jnp.int32(0)
        for core in range(2):
            dev = 2 * chip + core
            zt, xt = z_target(dev), x_target(dev)
            for b in range(nb):
                bits = live[dev * nb + b]
                zsum = zsum + popcount(bits & zt)
                xsum = xsum + popcount(bits & xt)
        xsum = jnp.where(lax.rem(chip, 2) == 1, xsum, 0)
        return jnp.maximum(most, jnp.maximum(zsum, xsum))

    nums[4] = lax.fori_loop(0, n // 2, chip_counts, jnp.int32(0))

    own = union[l]

    def build(first, z, out, coded, base=0):
        def panel(jj, at):
            dev = first + jj // nb
            b = lax.rem(jj, nb)
            j = dev * nb + b
            target = jnp.where(z, z_target(dev), x_target(dev))
            need = live[j] & target
            start = meta[2 * j]
            shift = dev - l

            def slot(p, at):
                tip = start + p
                tip = jnp.where(tip >= tips, tip - tips, tip)
                if coded:
                    good = (shift >= 0) & (shift <= SHIFTS) & ((srl(own, tip) & 1) == 1)
                    out[at + base] = jnp.where(good, jj * tips + tip, -1)
                else:
                    out[at] = jj * slots + p
                return at + (srl(need, tip) & 1)

            return lax.fori_loop(0, meta[2 * j + 1], slot, at)

        return lax.fori_loop(0, 2 * nb, panel, jnp.int32(0))

    mine = 2 * xcol
    nums[0] = build(mine, True, zsend, False)
    nums[1] = build(mine, False, xsend, False)
    nums[2] = build(ROW + mine, True, codes, True)
    nums[3] = build(jnp.where(xcol == 0, 2, ROW), xcol == 1, codes, True, codes.shape[0] // 2)


def pack_kernel(pieces, nb, slots, where, zsend, xsend, nums, own, peer, *rest):
    outs, sems = rest[:-1], rest[-1]
    core = where[2]

    def issue(todo, listed, count, start, out, sem):
        def one(s, _):
            e = listed[2 * (s + start) + core]
            jj = e // slots
            p = lax.rem(e, slots)
            b = lax.rem(jj, nb)
            mine = (jj // nb) == core
            for source, yes in ((own, mine), (peer, jnp.logical_not(mine))):

                @pl.when(yes)
                def _():
                    copy = pltpu.make_async_copy(source.at[:, b, p], out.at[s], sem.at[s])
                    copy.start() if todo else copy.wait()

            return 0

        held = jnp.clip((count - core + 1) // 2 - start, 0, out.shape[0])
        lax.fori_loop(0, held, one, 0)

    for todo in (True, False):
        for i, ((is_x, start), out) in enumerate(zip(pieces, outs)):
            count = jnp.where(where[1] == 1, nums[1], 0) if is_x else nums[0]
            issue(todo, xsend if is_x else zsend, count, start, out, sems.at[i])


def product(left, tile):
    flat = tile.reshape(tile.shape[0] * tile.shape[1], tile.shape[2])
    return jnp.dot(left, flat, preferred_element_type=jnp.float32)


def add_to(acc, kb, got):
    nf, nb, _, rows, _ = acc.shape
    for a in range(nb):
        for h in range(nf):
            at = (a * nf + h) * rows
            acc[h, a, kb] += got[at : at + rows]


def run_list(count, group, entry, left, acc):
    def some(i, _):
        found = [entry(group * i + g) for g in range(group)]
        got = [product(left[t], tile) for t, tile, _ in found]
        for (_, _, kb), part in zip(found, got):
            add_to(acc, kb, part)
        return 0

    lax.fori_loop(0, (count + group - 1) // group, some, 0)


def own_kernel(nb, tips, meta, raw, resid, left, acc, grad):
    freqs, width = raw.shape[0], raw.shape[-1]
    acc[...] = jnp.zeros_like(acc)
    grad[...] = jnp.zeros_like(grad)

    def turn(t, _):
        for a in range(nb):
            start, count = meta[2 * a], meta[2 * a + 1]
            p = t - start
            p = jnp.where(p < 0, p + tips, p)

            @pl.when(p < count)
            def _():
                for f in range(freqs):
                    left[t, pl.ds(a * width, width), pl.ds(f * width, width)] = raw[f, a, p].T

            @pl.when(p >= count)
            def _():
                left[t, pl.ds(a * width, width), :] = jnp.zeros(
                    (width, freqs * width), left.dtype
                )

        return 0

    lax.fori_loop(0, tips, turn, 0)

    left[tips] = jnp.zeros(left.shape[1:], left.dtype)
    for b in range(nb):
        start, count = meta[2 * b], meta[2 * b + 1]

        def one(i, _):
            for g in range(GROUP):
                p = GROUP * i + g
                t = start + p
                t = jnp.where(t >= tips, t - tips, t)
                t = jnp.where(p < count, t, tips)
                tile = raw[:, b, jnp.minimum(p, count - 1)]
                add_to(acc, b, product(left[t], tile))
                grad[b] += product(resid[t], tile)
            return 0

        lax.fori_loop(0, (count + GROUP - 1) // GROUP, one, 0)


def peer_kernel(tips, where, meta, left, raw, acc):
    acc[...] = jnp.zeros_like(acc)

    @pl.when(where[2] == 0)
    def _():
        nb = raw.shape[1]

        def panel(b, _):
            start, count = meta[2 * (nb + b)], meta[2 * (nb + b) + 1]

            def entry(p):
                t = start + p
                t = jnp.where(t >= tips, t - tips, t)
                t = jnp.where(p < count, t, tips)
                return t, raw[:, b, jnp.minimum(p, count - 1)], b

            run_list(count, GROUP, entry, left, acc)
            return 0

        lax.fori_loop(0, nb, panel, 0)


def chunk_kernel(tips, spans, first, where, codes, nums, left, *rest):
    held_in = rest[0] if not first else None
    arrays = rest[(0 if first else 1) : -3]
    acc, tiles, sems = rest[-3:]
    core = where[2]
    copies = []
    place = 0
    places = []
    for i, array in enumerate(arrays):
        size = array.shape[0]
        copies.append(pltpu.make_async_copy(array, tiles.at[pl.ds(place, size)], sems.at[i]))
        places.append((place, size))
        place += size
    for copy in copies:
        copy.start()
    if first:
        acc[...] = jnp.zeros_like(acc)
    else:
        acc[...] = held_in[...]
    for copy in copies:
        copy.wait()
    columns = acc.shape[2] // 2

    def array(q, _):
        def pick(values):
            got = jnp.int32(values[0])
            for i, v in enumerate(values[1:], 1):
                got = jnp.where(q == i, v, got)
            return got

        is_b = pick([int(b) for b, _, _ in spans])
        other = pick([int(o) for _, o, _ in spans])
        offset = pick([o for _, _, o in spans])
        place = pick([p for p, _ in places])
        size = pick([z for _, z in places])
        holder = jnp.where(other == 1, 1 - core, core)
        count = jnp.where(is_b == 1, nums[3], nums[2])
        held = jnp.clip((count - holder + 1) // 2 - offset, 0, size)
        base = is_b * (codes.shape[0] // 2) + 2 * offset + holder

        def entry(s):
            at = jnp.minimum(s, held - 1)
            code = codes[2 * at + base]
            good = (code >= 0) & (s < held)
            t = jnp.where(good, lax.rem(code, tips), tips)
            column = jnp.where(good, code // tips, columns - 1) + is_b * columns
            return t, tiles[place + at], column

        run_list(held, GROUP, entry, left, acc)
        return 0

    lax.fori_loop(0, len(spans), array, 0)


def call(kernel, outs, specs, out_specs, scratch=(), name=None, cost_us=0):
    return pl.pallas_call(
        kernel,
        out_shape=outs,
        in_specs=specs,
        out_specs=out_specs,
        scratch_shapes=scratch,
        name=name,
        cost_estimate=pl.CostEstimate(
            flops=int(cost_us * 1e9), transcendentals=0, bytes_accessed=int(cost_us * 1e6)
        ),
        compiler_params=pltpu.CompilerParams(vmem_limit_bytes=60000 * 1024),
    )


def on_device(tiles, tip_lists, counts, residual):
    freqs, nb, slots, width = tiles.shape[:4]
    tips = residual.shape[1] // width
    n = lax.axis_size("cells")
    nf = lax.axis_size("freq")
    rows = width // nf
    d = lax.axis_index("cells").astype(jnp.int32)
    fi = lax.axis_index("freq")
    i32 = jnp.int32

    def moved(x, to):
        return lax.ppermute(x, "cells", [(i, to(i) % n) for i in range(n)])

    peer = moved(tiles, lambda i: i ^ 1)

    own_meta = jnp.stack([tip_lists[:, 0], counts], axis=1).reshape(-1).astype(i32)
    meta = own_meta
    have = 1
    while have < n:
        more = moved(meta, lambda i: i - have)
        take = min(have, n - have) * 2 * nb
        meta = jnp.concatenate([meta, more[:take]])
        have = min(2 * have, n)
    l = lax.rem(d, i32(ROW))
    xcol = lax.rem(d // 2, i32(2))
    core = lax.rem(d, i32(2))
    where = jnp.stack([l, xcol, core])
    per = 2 * nb
    row_meta = lax.dynamic_slice(
        jnp.concatenate([meta, meta]), (lax.rem(n - l, i32(n)) * per,), (n * per,)
    )

    ints = lambda m: jax.ShapeDtypeStruct((m,), i32)
    room = 2 * nb * slots + 8
    zsend, xsend, codes, nums = call(
        functools.partial(list_kernel, n, nb, slots, tips),
        (ints(room), ints(room), ints(2 * room), ints(8)),
        [SMEM] * 2,
        (SMEM,) * 4,
        [pltpu.SMEM((n * nb,), i32), pltpu.SMEM((n,), i32)],
        name="lists",
        cost_us=6,
    )(where, row_meta)

    resid = residual.reshape(freqs, tips, width).transpose(1, 0, 2).reshape(tips, 1, freqs * width)
    resid = jnp.pad(
        jnp.broadcast_to(resid, (tips, 16, freqs * width)), ((0, 1), (0, 0), (0, 0))
    )

    def sums(columns):
        return jax.ShapeDtypeStruct((nf, nb, columns, rows, width), jnp.float32)

    def joined(x):
        got = lax.dynamic_index_in_dim(x, fi, 0, keepdims=False)
        for s in range(1, nf):
            part = lax.dynamic_index_in_dim(x, lax.rem(fi + s, nf), 0, keepdims=False)
            pairs = [(i, (i + s) % nf) for i in range(nf)]
            got = got + lax.ppermute(part, "freq", pairs)
        return got

    def pack(pieces):
        shapes = tuple(
            jax.ShapeDtypeStruct((end - at, freqs, width, width), tiles.dtype)
            for _, at, end in pieces
        )
        return call(
            functools.partial(pack_kernel, [p[:2] for p in pieces], nb, slots),
            shapes,
            [SMEM] * 4 + [ANY] * 2,
            (VMEM,) * len(shapes),
            [pltpu.SemaphoreType.DMA((len(shapes), max(x.shape[0] for x in shapes)))],
            name="pack",
            cost_us=6,
        )(where, zsend, xsend, nums, tiles, peer)

    def chunk(pieces, total):
        spans = [s for s, _ in pieces]
        arrays = [x for _, x in pieces]
        first = total is None
        specs = [SMEM] * 3 + [VMEM] * (1 if first else 2) + [ANY] * len(arrays)
        scratch = [
            pltpu.VMEM((sum(x.shape[0] for x in arrays), freqs, width, width), tiles.dtype),
            pltpu.SemaphoreType.DMA((len(arrays),)),
        ]
        more = () if first else (total,)
        return lambda left: call(
            functools.partial(chunk_kernel, tips, spans, first),
            sums(2 * (2 * nb + 1)),
            specs,
            VMEM,
            scratch,
            name="chunk",
            cost_us=14,
        )(where, codes, nums, left, *more, *arrays)

    def main(cuts):
        spots = list(zip((0,) + cuts, cuts))
        zpack = list(pack([(False,) + spots[0]]))
        rest = [(False,) + s for s in spots[1:]] + [(True,) + s for s in spots]
        later = pack(rest)
        zpack += later[: len(spots) - 1]
        xpack = later[len(spots) - 1 :]
        landed = [moved(z, lambda i: i - ROW) for z in zpack]
        my_tiles, _ = lax.optimization_barrier((tiles, later))
        left, own, grad = call(
            functools.partial(own_kernel, nb, tips),
            (
                jax.ShapeDtypeStruct((tips + 1, nb * width, freqs * width), tiles.dtype),
                sums(nb),
                jax.ShapeDtypeStruct((nb, 16, width), jnp.float32),
            ),
            [SMEM, VMEM, VMEM],
            (VMEM, VMEM, VMEM),
            name="own",
            cost_us=25,
        )(own_meta, my_tiles, resid)
        gate = own
        total = None
        ready = []
        peers = None
        for i, (at, end) in enumerate(spots):
            a, gate = lax.optimization_barrier((landed[i], gate))
            b = moved(jnp.where(xcol == 0, a, xpack[i]), lambda i: i ^ 2)
            a_peer = moved(a, lambda i: i ^ 1)
            b_peer = moved(b, lambda i: i ^ 1)
            ready += [((False, False, at), a), ((False, True, at), a_peer)]
            if i == 0:
                peers = gate = call(
                    functools.partial(peer_kernel, tips),
                    sums(nb),
                    [SMEM, SMEM, VMEM, VMEM],
                    VMEM,
                    name="peer",
                    cost_us=12,
                )(where, meta, left, peer)
                early = joined(jnp.concatenate([own, peers], axis=2))
                grad = grad[:, 0, :]
                grad_sum = grad
                for s in range(1, nf):
                    pairs = [(i, (i + s) % nf) for i in range(nf)]
                    grad_sum = grad_sum + lax.ppermute(grad, "freq", pairs)
            else:
                gate = total = chunk(ready, total)(left)
                ready = []
            ready += [((True, False, at), b), ((True, True, at), b_peer)]
        firsts = joined(total[:, :, : 2 * nb])
        total = chunk(ready, total)(left)
        seconds = joined(total[:, :, 2 * nb + 1 : 4 * nb + 1])
        all_of = jnp.concatenate([early, seconds, firsts], axis=1)
        own_part, rest = all_of[:, :nb], all_of[:, nb:]
        columns = SHIFTS * nb
        rest = jnp.where(core == 0, rest[:, :columns], rest[:, nb : nb + columns])
        band = jnp.concatenate([own_part, rest], axis=1)
        return band, grad_sum

    full = nb * slots
    levels = [full * m // 60 for m in LEVELS] + [full]
    need = (nums[4] + 1) // 2
    level = sum((need > h).astype(i32) for h in levels[:-1])

    def cuts_of(half):
        return tuple(half * m // 36 for m in CUTS)

    band, grad = lax.switch(level, [functools.partial(main, cuts_of(h)) for h in levels])
    return (
        band.reshape(nb, SHIFTS + 1, nb, rows, width),
        grad.reshape(nb * width),
    )


def solution(mesh):
    placed = (P("freq", "cells", None, None, None), P("cells", None), P("cells"), P("freq", None))
    return jax.shard_map(
        on_device,
        mesh=mesh,
        in_specs=placed,
        out_specs=(P("cells", None, None, "freq", None), P("cells")),
        check_vma=False,
    )
```

```python
import functools

import jax
import jax.numpy as jnp
from jax import lax
from jax.experimental import pallas as pl
from jax.experimental.pallas import tpu as pltpu
from jax.sharding import PartitionSpec as P


SHIFTS = 4
GROUP = 2
ROW = 4

LEVELS = (31, 34, 37, 40, 43, 48)
CUTS = (6, 14, 23, 31, 38, 43)
EVERY = 1

SMEM = pl.BlockSpec(memory_space=pltpu.SMEM)
VMEM = pl.BlockSpec(memory_space=pltpu.VMEM)
ANY = pl.BlockSpec(memory_space=pl.ANY)


def popcount(x):
    srl = lax.shift_right_logical
    x = x - (srl(x, jnp.int32(1)) & 0x55555555)
    x = (x & 0x33333333) + (srl(x, jnp.int32(2)) & 0x33333333)
    x = (x + srl(x, jnp.int32(4))) & 0x0F0F0F0F
    x = x + srl(x, jnp.int32(8))
    x = x + srl(x, jnp.int32(16))
    return x & 63


def list_kernel(n, nb, slots, tips, where, meta, zsend, xsend, codes, nums, live, union):
    srl = lax.shift_right_logical
    l, xcol = where[0], where[1]

    def fill(dev, _):
        total = jnp.int32(0)
        for b in range(nb):
            j = dev * nb + b
            start, count = meta[2 * j], meta[2 * j + 1]
            ones = (jnp.int32(1) << count) - 1
            bits = (ones << start) | srl(srl(ones, tips - 1 - start), jnp.int32(1))
            if tips < 32:
                bits = bits & ((1 << tips) - 1)
            live[j] = bits
            total = total | bits
        union[dev] = total
        return 0

    lax.fori_loop(0, n, fill, 0)

    def wrap(dev):
        return lax.rem(dev + n, n)

    def z_target(dev):
        base = (dev // ROW) * ROW
        at = dev - base
        total = union[wrap(base - 1)]
        for back in range(2, ROW + 1):
            got = union[wrap(base - back)]
            total = total | jnp.where(ROW - back >= at, got, 0)
        return total

    def x_target(dev):
        base = (dev // ROW) * ROW
        return union[base] | union[base + 1]

    def chip_counts(chip, most):
        zsum, xsum = jnp.int32(0), jnp.int32(0)
        for core in range(2):
            dev = 2 * chip + core
            zt, xt = z_target(dev), x_target(dev)
            for b in range(nb):
                bits = live[dev * nb + b]
                zsum = zsum + popcount(bits & zt)
                xsum = xsum + popcount(bits & xt)
        xsum = jnp.where(lax.rem(chip, 2) == 1, xsum, 0)
        return jnp.maximum(most, jnp.maximum(zsum, xsum))

    nums[4] = lax.fori_loop(0, n // 2, chip_counts, jnp.int32(0))

    own = union[l]

    def build(first, z, out, coded, base=0):
        def panel(jj, at):
            dev = first + jj // nb
            b = lax.rem(jj, nb)
            j = dev * nb + b
            target = jnp.where(z, z_target(dev), x_target(dev))
            need = live[j] & target
            start = meta[2 * j]
            shift = dev - l

            def slot(p, at):
                tip = start + p
                tip = jnp.where(tip >= tips, tip - tips, tip)
                if coded:
                    good = (shift >= 0) & (shift <= SHIFTS) & ((srl(own, tip) & 1) == 1)
                    out[at + base] = jnp.where(good, jj * tips + tip, -1)
                else:
                    out[at] = jj * slots + p
                return at + (srl(need, tip) & 1)

            return lax.fori_loop(0, meta[2 * j + 1], slot, at)

        return lax.fori_loop(0, 2 * nb, panel, jnp.int32(0))

    mine = 2 * xcol
    nums[0] = build(mine, True, zsend, False)
    nums[1] = build(mine, False, xsend, False)
    nums[2] = build(ROW + mine, True, codes, True)
    nums[3] = build(jnp.where(xcol == 0, 2, ROW), xcol == 1, codes, True, codes.shape[0] // 2)


def pack_kernel(pieces, nb, slots, where, zsend, xsend, nums, own, peer, *rest):
    outs, sems = rest[:-1], rest[-1]
    core = where[2]

    def issue(todo, listed, count, start, out, sem):
        def one(s, _):
            e = listed[2 * (s + start) + core]
            jj = e // slots
            p = lax.rem(e, slots)
            b = lax.rem(jj, nb)
            mine = (jj // nb) == core
            for source, yes in ((own, mine), (peer, jnp.logical_not(mine))):

                @pl.when(yes)
                def _():
                    copy = pltpu.make_async_copy(source.at[:, b, p], out.at[s], sem.at[s])
                    copy.start() if todo else copy.wait()

            return 0

        held = jnp.clip((count - core + 1) // 2 - start, 0, out.shape[0])
        lax.fori_loop(0, held, one, 0)

    for todo in (True, False):
        for i, ((is_x, start), out) in enumerate(zip(pieces, outs)):
            count = jnp.where(where[1] == 1, nums[1], 0) if is_x else nums[0]
            issue(todo, xsend if is_x else zsend, count, start, out, sems.at[i])


def product(left, tile):
    flat = tile.reshape(tile.shape[0] * tile.shape[1], tile.shape[2])
    return jnp.dot(left, flat, preferred_element_type=jnp.float32)


def add_to(acc, kb, got):
    nf, nb, _, rows, _ = acc.shape
    for a in range(nb):
        for h in range(nf):
            at = (a * nf + h) * rows
            acc[h, a, kb] += got[at : at + rows]


def run_list(count, group, entry, left, acc):
    def some(i, _):
        found = [entry(group * i + g) for g in range(group)]
        got = [product(left[t], tile) for t, tile, _ in found]
        for (_, _, kb), part in zip(found, got):
            add_to(acc, kb, part)
        return 0

    lax.fori_loop(0, (count + group - 1) // group, some, 0)


def own_kernel(nb, tips, meta, raw, resid, left, acc, grad):
    freqs, width = raw.shape[0], raw.shape[-1]
    acc[...] = jnp.zeros_like(acc)
    grad[...] = jnp.zeros_like(grad)

    def turn(t, _):
        for a in range(nb):
            start, count = meta[2 * a], meta[2 * a + 1]
            p = t - start
            p = jnp.where(p < 0, p + tips, p)

            @pl.when(p < count)
            def _():
                for f in range(freqs):
                    left[t, pl.ds(a * width, width), pl.ds(f * width, width)] = raw[f, a, p].T

            @pl.when(p >= count)
            def _():
                left[t, pl.ds(a * width, width), :] = jnp.zeros(
                    (width, freqs * width), left.dtype
                )

        return 0

    lax.fori_loop(0, tips, turn, 0)

    left[tips] = jnp.zeros(left.shape[1:], left.dtype)
    for b in range(nb):
        start, count = meta[2 * b], meta[2 * b + 1]

        def one(i, _):
            for g in range(GROUP):
                p = GROUP * i + g
                t = start + p
                t = jnp.where(t >= tips, t - tips, t)
                t = jnp.where(p < count, t, tips)
                tile = raw[:, b, jnp.minimum(p, count - 1)]
                add_to(acc, b, product(left[t], tile))
                grad[b] += product(resid[t], tile)
            return 0

        lax.fori_loop(0, (count + GROUP - 1) // GROUP, one, 0)


def peer_kernel(tips, where, meta, left, raw, acc):
    acc[...] = jnp.zeros_like(acc)

    @pl.when(where[2] == 0)
    def _():
        nb = raw.shape[1]

        def panel(b, _):
            start, count = meta[2 * (nb + b)], meta[2 * (nb + b) + 1]

            def entry(p):
                t = start + p
                t = jnp.where(t >= tips, t - tips, t)
                t = jnp.where(p < count, t, tips)
                return t, raw[:, b, jnp.minimum(p, count - 1)], b

            run_list(count, GROUP, entry, left, acc)
            return 0

        lax.fori_loop(0, nb, panel, 0)


def chunk_kernel(tips, spans, first, where, codes, nums, left, *rest):
    held_in = rest[0] if not first else None
    arrays = rest[(0 if first else 1) : -3]
    acc, tiles, sems = rest[-3:]
    core = where[2]
    copies = []
    place = 0
    places = []
    for i, array in enumerate(arrays):
        size = array.shape[0]
        copies.append(pltpu.make_async_copy(array, tiles.at[pl.ds(place, size)], sems.at[i]))
        places.append((place, size))
        place += size
    for copy in copies:
        copy.start()
    if first:
        acc[...] = jnp.zeros_like(acc)
    else:
        acc[...] = held_in[...]
    for copy in copies:
        copy.wait()
    columns = acc.shape[2] // 2

    def array(q, _):
        def pick(values):
            got = jnp.int32(values[0])
            for i, v in enumerate(values[1:], 1):
                got = jnp.where(q == i, v, got)
            return got

        is_b = pick([int(b) for b, _, _ in spans])
        other = pick([int(o) for _, o, _ in spans])
        offset = pick([o for _, _, o in spans])
        place = pick([p for p, _ in places])
        size = pick([z for _, z in places])
        holder = jnp.where(other == 1, 1 - core, core)
        count = jnp.where(is_b == 1, nums[3], nums[2])
        held = jnp.clip((count - holder + 1) // 2 - offset, 0, size)
        base = is_b * (codes.shape[0] // 2) + 2 * offset + holder

        def entry(s):
            at = jnp.minimum(s, held - 1)
            code = codes[2 * at + base]
            good = (code >= 0) & (s < held)
            t = jnp.where(good, lax.rem(code, tips), tips)
            column = jnp.where(good, code // tips, columns - 1) + is_b * columns
            return t, tiles[place + at], column

        run_list(held, GROUP, entry, left, acc)
        return 0

    lax.fori_loop(0, len(spans), array, 0)


def add_kernel(*refs):
    total = refs[0][...]
    for ref in refs[1:-1]:
        total = total + ref[...]
    refs[-1][...] = total


def call(kernel, outs, specs, out_specs, scratch=(), cost_us=0):
    return pl.pallas_call(
        kernel,
        out_shape=outs,
        in_specs=specs,
        out_specs=out_specs,
        scratch_shapes=scratch,
        cost_estimate=pl.CostEstimate(
            flops=int(cost_us * 1e9), transcendentals=0, bytes_accessed=int(cost_us * 1e6)
        ),
        compiler_params=pltpu.CompilerParams(vmem_limit_bytes=32000 * 1024),
    )


def on_device(tiles, tip_lists, counts, residual):
    freqs, nb, slots, width = tiles.shape[:4]
    tips = residual.shape[1] // width
    n = lax.axis_size("cells")
    nf = lax.axis_size("freq")
    rows = width // nf
    d = lax.axis_index("cells").astype(jnp.int32)
    fi = lax.axis_index("freq")
    i32 = jnp.int32

    def moved(x, to):
        return lax.ppermute(x, "cells", [(i, to(i) % n) for i in range(n)])

    own_meta = jnp.stack([tip_lists[:, 0], counts], axis=1).reshape(-1).astype(i32)
    meta = own_meta
    have = 1
    peer = None
    while have < n:
        steps = [k for k in range(1, ROW) if k * have < n]
        got = [moved(meta, lambda i, k=k: i - k * have) for k in steps]
        if have == 1:
            *got, hold = lax.optimization_barrier((*got, tiles))
            peer = moved(hold, lambda i: i ^ 1)
        meta = jnp.concatenate(
            [meta] + [x[: min(have, n - k * have) * 2 * nb] for k, x in zip(steps, got)]
        )
        have = meta.shape[0] // (2 * nb)
    l = lax.rem(d, i32(ROW))
    xcol = lax.rem(d // 2, i32(2))
    core = lax.rem(d, i32(2))
    where = jnp.stack([l, xcol, core])
    per = 2 * nb
    row_meta = lax.dynamic_slice(
        jnp.concatenate([meta, meta]), (lax.rem(n - l, i32(n)) * per,), (n * per,)
    )

    ints = lambda m: jax.ShapeDtypeStruct((m,), i32)
    room = 2 * nb * slots + 8
    zsend, xsend, codes, nums = call(
        functools.partial(list_kernel, n, nb, slots, tips),
        (ints(room), ints(room), ints(2 * room), ints(8)),
        [SMEM] * 2,
        (SMEM,) * 4,
        [pltpu.SMEM((n * nb,), i32), pltpu.SMEM((n,), i32)],
        cost_us=6,
    )(where, row_meta)

    resid = residual.reshape(freqs, tips, width).transpose(1, 0, 2).reshape(tips, 1, freqs * width)
    resid = jnp.pad(
        jnp.broadcast_to(resid, (tips, 16, freqs * width)), ((0, 1), (0, 0), (0, 0))
    )

    def sums(columns):
        return jax.ShapeDtypeStruct((nf, nb, columns, rows, width), jnp.float32)

    def joined(x):
        got = lax.dynamic_index_in_dim(x, fi, 0, keepdims=False)
        for s in range(1, nf):
            part = lax.dynamic_index_in_dim(x, lax.rem(fi + s, nf), 0, keepdims=False)
            pairs = [(i, (i + s) % nf) for i in range(nf)]
            got = got + lax.ppermute(part, "freq", pairs)
        return got

    def pack(pieces):
        shapes = tuple(
            jax.ShapeDtypeStruct((end - at, freqs, width, width), tiles.dtype)
            for _, at, end in pieces
        )
        return call(
            functools.partial(pack_kernel, [p[:2] for p in pieces], nb, slots),
            shapes,
            [SMEM] * 4 + [ANY] * 2,
            (VMEM,) * len(shapes),
            [pltpu.SemaphoreType.DMA((len(shapes), max(x.shape[0] for x in shapes)))],
            cost_us=6,
        )(where, zsend, xsend, nums, tiles, peer)

    def chunk(pieces, total):
        spans = [s for s, _ in pieces]
        arrays = [x for _, x in pieces]
        first = total is None
        specs = [SMEM] * 3 + [VMEM] * (1 if first else 2) + [ANY] * len(arrays)
        scratch = [
            pltpu.VMEM((sum(x.shape[0] for x in arrays), freqs, width, width), tiles.dtype),
            pltpu.SemaphoreType.DMA((len(arrays),)),
        ]
        more = () if first else (total,)
        return lambda left: call(
            functools.partial(chunk_kernel, tips, spans, first),
            sums(2 * (2 * nb + 1)),
            specs,
            VMEM,
            scratch,
            cost_us=14,
        )(where, codes, nums, left, *more, *arrays)

    def main(cuts):
        return parts(cuts)

    def parts(cuts):
        spots = list(zip((0,) + cuts, cuts))
        zpack = list(pack([(False,) + spots[0]]))
        rest = [(False,) + s for s in spots[1:]] + [(True,) + s for s in spots]
        later = pack(rest)
        zpack += later[: len(spots) - 1]
        xpack = later[len(spots) - 1 :]
        landed = [moved(z, lambda i: i - ROW) for z in zpack]
        left, own, grad = call(
            functools.partial(own_kernel, nb, tips),
            (
                jax.ShapeDtypeStruct((tips + 1, nb * width, freqs * width), tiles.dtype),
                sums(nb),
                jax.ShapeDtypeStruct((nb, 16, width), jnp.float32),
            ),
            [SMEM, VMEM, VMEM],
            (VMEM, VMEM, VMEM),
            cost_us=25,
        )(own_meta, tiles, resid)
        gate = own
        total = None
        ready = []
        peers = None
        for i, (at, end) in enumerate(spots):
            a = landed[i]
            if i > 1:
                a, gate = lax.optimization_barrier((a, gate))
            b = moved(jnp.where(xcol == 0, a, xpack[i]), lambda i: i ^ 2)
            a_peer = moved(a, lambda i: i ^ 1)
            ready += [((False, False, at), a), ((False, True, at), a_peer)]
            if i == 0:
                peers = gate = call(
                    functools.partial(peer_kernel, tips),
                    sums(nb),
                    [SMEM, SMEM, VMEM, VMEM],
                    VMEM,
                    cost_us=12,
                )(where, meta, left, peer)
                early = joined(jnp.concatenate([own, peers], axis=2))
                grad = grad[:, 0, :]
                grads = [grad]
                for s in range(1, nf):
                    pairs = [(i, (i + s) % nf) for i in range(nf)]
                    grads.append(lax.ppermute(grad, "freq", pairs))
                grad_sum = call(
                    add_kernel,
                    jax.ShapeDtypeStruct(grad.shape, grad.dtype),
                    [VMEM] * nf,
                    VMEM,
                    cost_us=1,
                )(*grads)
            elif (len(spots) - 1 - i) % EVERY == 0:
                gate = total = chunk(ready, total)(left)
                ready = []
            b, gate = lax.optimization_barrier((b, gate))
            b_peer = moved(b, lambda i: i ^ 1)
            ready += [((True, False, at), b), ((True, True, at), b_peer)]
        firsts = joined(total[:, :, : 2 * nb])
        total = chunk(ready, total)(left)
        seconds = joined(total[:, :, 2 * nb + 1 : 4 * nb + 1])
        all_of = jnp.concatenate([early, seconds, firsts], axis=1)
        own_part, rest = all_of[:, :nb], all_of[:, nb:]
        columns = SHIFTS * nb
        rest = jnp.where(core == 0, rest[:, :columns], rest[:, nb : nb + columns])
        band = jnp.concatenate([own_part, rest], axis=1)
        return band, grad_sum

    full = nb * slots
    levels = [full * m // 60 for m in LEVELS] + [full]
    need = (nums[4] + 1) // 2
    level = sum((need > h).astype(i32) for h in levels[:-1])

    def cuts_of(half):
        return tuple(half * m // CUTS[-1] for m in CUTS)

    band, grad = lax.switch(level, [functools.partial(main, cuts_of(h)) for h in levels])
    return (
        band.reshape(nb, SHIFTS + 1, nb, rows, width),
        grad.reshape(nb * width),
    )


def solution(mesh):
    placed = (P("freq", "cells", None, None, None), P("cells", None), P("cells"), P("freq", None))
    return jax.shard_map(
        on_device,
        mesh=mesh,
        in_specs=placed,
        out_specs=(P("cells", None, None, "freq", None), P("cells")),
        check_vma=False,
    )
```

```python
import functools

import jax
import jax.numpy as jnp
from jax import lax
from jax.experimental import pallas as pl
from jax.experimental.pallas import tpu as pltpu
from jax.sharding import PartitionSpec as P


SHIFTS = 4
GROUP = 1
ROW = 4

LEVELS = (36, 40, 45)
CUTS = (6, 16, 27, 36, 43)
EVERY = 1

SMEM = pl.BlockSpec(memory_space=pltpu.SMEM)
VMEM = pl.BlockSpec(memory_space=pltpu.VMEM)
ANY = pl.BlockSpec(memory_space=pl.ANY)


def popcount(x):
    srl = lax.shift_right_logical
    x = x - (srl(x, jnp.int32(1)) & 0x55555555)
    x = (x & 0x33333333) + (srl(x, jnp.int32(2)) & 0x33333333)
    x = (x + srl(x, jnp.int32(4))) & 0x0F0F0F0F
    x = x + srl(x, jnp.int32(8))
    x = x + srl(x, jnp.int32(16))
    return x & 63


def list_kernel(n, nb, slots, tips, where, meta, zsend, xsend, codes, nums, live, union):
    srl = lax.shift_right_logical
    l, xcol = where[0], where[1]

    def fill(dev, _):
        total = jnp.int32(0)
        for b in range(nb):
            j = dev * nb + b
            start, count = meta[2 * j], meta[2 * j + 1]
            ones = (jnp.int32(1) << count) - 1
            bits = (ones << start) | srl(srl(ones, tips - 1 - start), jnp.int32(1))
            if tips < 32:
                bits = bits & ((1 << tips) - 1)
            live[j] = bits
            total = total | bits
        union[dev] = total
        return 0

    lax.fori_loop(0, n, fill, 0)

    def wrap(dev):
        return lax.rem(dev + n, n)

    def z_target(dev):
        base = (dev // ROW) * ROW
        at = dev - base
        total = union[wrap(base - 1)]
        for back in range(2, ROW + 1):
            got = union[wrap(base - back)]
            total = total | jnp.where(ROW - back >= at, got, 0)
        return total

    def x_target(dev):
        base = (dev // ROW) * ROW
        return union[base] | union[base + 1]

    def chip_counts(chip, most):
        zsum, xsum = jnp.int32(0), jnp.int32(0)
        for core in range(2):
            dev = 2 * chip + core
            zt, xt = z_target(dev), x_target(dev)
            for b in range(nb):
                bits = live[dev * nb + b]
                zsum = zsum + popcount(bits & zt)
                xsum = xsum + popcount(bits & xt)
        xsum = jnp.where(lax.rem(chip, 2) == 1, xsum, 0)
        return jnp.maximum(most, jnp.maximum(zsum, xsum))

    nums[4] = lax.fori_loop(0, n // 2, chip_counts, jnp.int32(0))

    own = union[l]

    def build(first, z, out, coded, base=0):
        at = jnp.int32(0)
        for half in range(2):
            dev = first + half
            target = jnp.where(z, z_target(dev), x_target(dev))
            shift = dev - l
            near = (shift >= 0) & (shift <= SHIFTS)
            wanted = jnp.where(near, own, 0)
            for b in range(nb):
                j = dev * nb + b
                jj = half * nb + b
                need = live[j] & target
                start = meta[2 * j]

                def slot(p, at, jj=jj, start=start, need=need, wanted=wanted):
                    tip = start + p
                    tip = jnp.where(tip >= tips, tip - tips, tip)
                    if coded:
                        good = (srl(wanted, tip) & 1) == 1
                        out[at + base] = jnp.where(good, jj * tips + tip, -1)
                    else:
                        out[at] = jj * slots + p
                    return at + (srl(need, tip) & 1)

                at = lax.fori_loop(0, meta[2 * j + 1], slot, at)
        return at

    mine = 2 * xcol
    nums[0] = build(mine, True, zsend, False)
    nums[1] = build(mine, False, xsend, False)
    nums[2] = build(ROW + mine, True, codes, True)
    nums[3] = build(jnp.where(xcol == 0, 2, ROW), xcol == 1, codes, True, codes.shape[0] // 2)


def pack_kernel(pieces, nb, slots, where, zsend, xsend, nums, own, peer, *rest):
    outs, sems = rest[:-1], rest[-1]
    core = where[2]

    def issue(todo, listed, count, start, out, sem):
        def one(s, _):
            e = listed[2 * (s + start) + core]
            jj = e // slots
            p = lax.rem(e, slots)
            b = lax.rem(jj, nb)
            mine = (jj // nb) == core
            for source, yes in ((own, mine), (peer, jnp.logical_not(mine))):

                @pl.when(yes)
                def _():
                    copy = pltpu.make_async_copy(source.at[:, b, p], out.at[s], sem.at[s])
                    copy.start() if todo else copy.wait()

            return 0

        held = jnp.clip((count - core + 1) // 2 - start, 0, out.shape[0])
        lax.fori_loop(0, held, one, 0)

    for todo in (True, False):
        for i, ((is_x, start), out) in enumerate(zip(pieces, outs)):
            count = jnp.where(where[1] == 1, nums[1], 0) if is_x else nums[0]
            issue(todo, xsend if is_x else zsend, count, start, out, sems.at[i])


def product(left, tile):
    flat = tile.reshape(tile.shape[0] * tile.shape[1], tile.shape[2])
    return jnp.dot(left, flat, preferred_element_type=jnp.float32)


def add_to(acc, kb, got):
    nf, nb, _, rows, _ = acc.shape
    for a in range(nb):
        for h in range(nf):
            at = (a * nf + h) * rows
            acc[h, a, kb] += got[at : at + rows]


def run_list(count, group, entry, left, acc):
    def some(i, _):
        found = [entry(group * i + g) for g in range(group)]
        got = [product(left[t], tile) for t, tile, _ in found]
        for (_, _, kb), part in zip(found, got):
            add_to(acc, kb, part)
        return 0

    lax.fori_loop(0, (count + group - 1) // group, some, 0)


def own_kernel(nb, tips, meta, raw, resid, left, acc, grad):
    freqs, width = raw.shape[0], raw.shape[-1]
    acc[...] = jnp.zeros_like(acc)
    grad[...] = jnp.zeros_like(grad)

    def turn(t, _):
        for a in range(nb):
            start, count = meta[2 * a], meta[2 * a + 1]
            p = t - start
            p = jnp.where(p < 0, p + tips, p)

            @pl.when(p < count)
            def _():
                for f in range(freqs):
                    left[t, pl.ds(a * width, width), pl.ds(f * width, width)] = raw[f, a, p].T

            @pl.when(p >= count)
            def _():
                left[t, pl.ds(a * width, width), :] = jnp.zeros(
                    (width, freqs * width), left.dtype
                )

        return 0

    lax.fori_loop(0, tips, turn, 0)

    left[tips] = jnp.zeros(left.shape[1:], left.dtype)
    for b in range(nb):
        start, count = meta[2 * b], meta[2 * b + 1]

        def one(i, _):
            for g in range(GROUP):
                p = GROUP * i + g
                t = start + p
                t = jnp.where(t >= tips, t - tips, t)
                t = jnp.where(p < count, t, tips)
                tile = raw[:, b, jnp.minimum(p, count - 1)]
                add_to(acc, b, product(left[t], tile))
                grad[b] += product(resid[t], tile)
            return 0

        lax.fori_loop(0, (count + GROUP - 1) // GROUP, one, 0)


def peer_kernel(tips, where, meta, left, raw, acc):
    acc[...] = jnp.zeros_like(acc)

    @pl.when(where[2] == 0)
    def _():
        nb = raw.shape[1]

        def panel(b, _):
            start, count = meta[2 * (nb + b)], meta[2 * (nb + b) + 1]

            def entry(p):
                t = start + p
                t = jnp.where(t >= tips, t - tips, t)
                t = jnp.where(p < count, t, tips)
                return t, raw[:, b, jnp.minimum(p, count - 1)], b

            run_list(count, GROUP, entry, left, acc)
            return 0

        lax.fori_loop(0, nb, panel, 0)


def chunk_kernel(tips, spans, first, where, codes, nums, left, *rest):
    held_in = rest[0] if not first else None
    arrays = rest[(0 if first else 1) : -3]
    acc, tiles, sems = rest[-3:]
    core = where[2]
    copies = []
    place = 0
    places = []
    for i, array in enumerate(arrays):
        size = array.shape[0]
        copies.append(pltpu.make_async_copy(array, tiles.at[pl.ds(place, size)], sems.at[i]))
        places.append((place, size))
        place += size
    for copy in copies:
        copy.start()
    if first:
        acc[...] = jnp.zeros_like(acc)
    else:
        acc[...] = held_in[...]
    for copy in copies:
        copy.wait()
    columns = acc.shape[2] // 2

    def array(q, _):
        def pick(values):
            got = jnp.int32(values[0])
            for i, v in enumerate(values[1:], 1):
                got = jnp.where(q == i, v, got)
            return got

        is_b = pick([int(b) for b, _, _ in spans])
        other = pick([int(o) for _, o, _ in spans])
        offset = pick([o for _, _, o in spans])
        place = pick([p for p, _ in places])
        size = pick([z for _, z in places])
        holder = jnp.where(other == 1, 1 - core, core)
        count = jnp.where(is_b == 1, nums[3], nums[2])
        held = jnp.clip((count - holder + 1) // 2 - offset, 0, size)
        base = is_b * (codes.shape[0] // 2) + 2 * offset + holder

        def entry(s):
            at = jnp.minimum(s, held - 1)
            code = codes[2 * at + base]
            good = (code >= 0) & (s < held)
            t = jnp.where(good, lax.rem(code, tips), tips)
            column = jnp.where(good, code // tips, columns - 1) + is_b * columns
            return t, tiles[place + at], column

        run_list(held, GROUP, entry, left, acc)
        return 0

    lax.fori_loop(0, len(spans), array, 0)


def add_kernel(*refs):
    total = refs[0][...]
    for ref in refs[1:-1]:
        total = total + ref[...]
    refs[-1][...] = total


def call(kernel, outs, specs, out_specs, scratch=(), cost_us=0):
    return pl.pallas_call(
        kernel,
        out_shape=outs,
        in_specs=specs,
        out_specs=out_specs,
        scratch_shapes=scratch,
        cost_estimate=pl.CostEstimate(
            flops=int(cost_us * 1e9), transcendentals=0, bytes_accessed=int(cost_us * 1e6)
        ),
        compiler_params=pltpu.CompilerParams(vmem_limit_bytes=20000 * 1024),
    )


def on_device(tiles, tip_lists, counts, residual):
    freqs, nb, slots, width = tiles.shape[:4]
    tips = residual.shape[1] // width
    n = lax.axis_size("cells")
    nf = lax.axis_size("freq")
    rows = width // nf
    d = lax.axis_index("cells").astype(jnp.int32)
    fi = lax.axis_index("freq")
    i32 = jnp.int32

    def moved(x, to):
        return lax.ppermute(x, "cells", [(i, to(i) % n) for i in range(n)])

    own_meta = jnp.stack([tip_lists[:, 0], counts], axis=1).reshape(-1).astype(i32)
    meta = own_meta
    have = 1
    peer = None
    while have < n:
        steps = [k for k in range(1, ROW) if k * have < n]
        got = [moved(meta, lambda i, k=k: i - k * have) for k in steps]
        if have == 1:
            *got, hold = lax.optimization_barrier((*got, tiles))
            peer = moved(hold, lambda i: i ^ 1)
        meta = jnp.concatenate(
            [meta] + [x[: min(have, n - k * have) * 2 * nb] for k, x in zip(steps, got)]
        )
        have = meta.shape[0] // (2 * nb)
    l = lax.rem(d, i32(ROW))
    xcol = lax.rem(d // 2, i32(2))
    core = lax.rem(d, i32(2))
    where = jnp.stack([l, xcol, core])
    per = 2 * nb
    row_meta = lax.dynamic_slice(
        jnp.concatenate([meta, meta]), (lax.rem(n - l, i32(n)) * per,), (n * per,)
    )

    ints = lambda m: jax.ShapeDtypeStruct((m,), i32)
    room = 2 * nb * slots + 8
    zsend, xsend, codes, nums = call(
        functools.partial(list_kernel, n, nb, slots, tips),
        (ints(room), ints(room), ints(2 * room), ints(8)),
        [SMEM] * 2,
        (SMEM,) * 4,
        [pltpu.SMEM((n * nb,), i32), pltpu.SMEM((n,), i32)],
        cost_us=6,
    )(where, row_meta)

    resid = residual.reshape(freqs, tips, width).transpose(1, 0, 2).reshape(tips, 1, freqs * width)
    resid = jnp.pad(
        jnp.broadcast_to(resid, (tips, 16, freqs * width)), ((0, 1), (0, 0), (0, 0))
    )

    def sums(columns):
        return jax.ShapeDtypeStruct((nf, nb, columns, rows, width), jnp.float32)

    def joined(x):
        got = lax.dynamic_index_in_dim(x, fi, 0, keepdims=False)
        for s in range(1, nf):
            part = lax.dynamic_index_in_dim(x, lax.rem(fi + s, nf), 0, keepdims=False)
            pairs = [(i, (i + s) % nf) for i in range(nf)]
            got = got + lax.ppermute(part, "freq", pairs)
        return got

    def pack(pieces):
        shapes = tuple(
            jax.ShapeDtypeStruct((end - at, freqs, width, width), tiles.dtype)
            for _, at, end in pieces
        )
        return call(
            functools.partial(pack_kernel, [p[:2] for p in pieces], nb, slots),
            shapes,
            [SMEM] * 4 + [ANY] * 2,
            (VMEM,) * len(shapes),
            [pltpu.SemaphoreType.DMA((len(shapes), max(x.shape[0] for x in shapes)))],
            cost_us=6,
        )(where, zsend, xsend, nums, tiles, peer)

    def chunk(pieces, total):
        spans = [s for s, _ in pieces]
        arrays = [x for _, x in pieces]
        first = total is None
        specs = [SMEM] * 3 + [VMEM] * (1 if first else 2) + [ANY] * len(arrays)
        scratch = [
            pltpu.VMEM((sum(x.shape[0] for x in arrays), freqs, width, width), tiles.dtype),
            pltpu.SemaphoreType.DMA((len(arrays),)),
        ]
        more = () if first else (total,)
        return lambda left: call(
            functools.partial(chunk_kernel, tips, spans, first),
            sums(2 * (2 * nb + 1)),
            specs,
            VMEM,
            scratch,
            cost_us=14,
        )(where, codes, nums, left, *more, *arrays)

    def main(cuts):
        return parts(cuts)

    def parts(cuts):
        spots = list(zip((0,) + cuts, cuts))
        zpack = list(pack([(False,) + spots[0]]))
        rest = [(False,) + s for s in spots[1:]] + [(True,) + s for s in spots]
        later = pack(rest)
        zpack += later[: len(spots) - 1]
        xpack = later[len(spots) - 1 :]
        landed = [moved(z, lambda i: i - ROW) for z in zpack]
        left, own, grad = call(
            functools.partial(own_kernel, nb, tips),
            (
                jax.ShapeDtypeStruct((tips + 1, nb * width, freqs * width), tiles.dtype),
                sums(nb),
                jax.ShapeDtypeStruct((nb, 16, width), jnp.float32),
            ),
            [SMEM, VMEM, VMEM],
            (VMEM, VMEM, VMEM),
            cost_us=25,
        )(own_meta, tiles, resid)
        gate = own
        total = None
        ready = []
        peers = None
        for i, (at, end) in enumerate(spots):
            a = landed[i]
            if i > 1:
                a, gate = lax.optimization_barrier((a, gate))
            b = moved(jnp.where(xcol == 0, a, xpack[i]), lambda i: i ^ 2)
            a_peer = moved(a, lambda i: i ^ 1)
            ready += [((False, False, at), a), ((False, True, at), a_peer)]
            if i == 0:
                peers = gate = call(
                    functools.partial(peer_kernel, tips),
                    sums(nb),
                    [SMEM, SMEM, VMEM, VMEM],
                    VMEM,
                    cost_us=12,
                )(where, meta, left, peer)
                early = joined(jnp.concatenate([own, peers], axis=2))
                grad = grad[:, 0, :]
                grads = [grad]
                for s in range(1, nf):
                    pairs = [(i, (i + s) % nf) for i in range(nf)]
                    grads.append(lax.ppermute(grad, "freq", pairs))
                grad_sum = call(
                    add_kernel,
                    jax.ShapeDtypeStruct(grad.shape, grad.dtype),
                    [VMEM] * nf,
                    VMEM,
                    cost_us=1,
                )(*grads)
            elif (len(spots) - 1 - i) % EVERY == 0:
                gate = total = chunk(ready, total)(left)
                ready = []
            b, gate = lax.optimization_barrier((b, gate))
            b_peer = moved(b, lambda i: i ^ 1)
            ready += [((True, False, at), b), ((True, True, at), b_peer)]
        firsts = joined(total[:, :, : 2 * nb])
        total = chunk(ready, total)(left)
        seconds = joined(total[:, :, 2 * nb + 1 : 4 * nb + 1])
        all_of = jnp.concatenate([early, seconds, firsts], axis=1)
        own_part, rest = all_of[:, :nb], all_of[:, nb:]
        columns = SHIFTS * nb
        rest = jnp.where(core == 0, rest[:, :columns], rest[:, nb : nb + columns])
        band = jnp.concatenate([own_part, rest], axis=1)
        return band, grad_sum

    full = nb * slots
    levels = [full * m // 60 for m in LEVELS] + [full]
    need = (nums[4] + 1) // 2
    level = sum((need > h).astype(i32) for h in levels[:-1])

    def cuts_of(half):
        return tuple(half * m // CUTS[-1] for m in CUTS)

    band, grad = lax.switch(level, [functools.partial(main, cuts_of(h)) for h in levels])
    return (
        band.reshape(nb, SHIFTS + 1, nb, rows, width),
        grad.reshape(nb * width),
    )


def solution(mesh):
    placed = (P("freq", "cells", None, None, None), P("cells", None), P("cells"), P("freq", None))
    return jax.shard_map(
        on_device,
        mesh=mesh,
        in_specs=placed,
        out_specs=(P("cells", None, None, "freq", None), P("cells")),
        check_vma=False,
    )
```

```python
import functools

import jax
import jax.numpy as jnp
from jax import lax
from jax.experimental import pallas as pl
from jax.experimental.pallas import tpu as pltpu
from jax.sharding import PartitionSpec as P


SHIFTS = 4
GROUP = 1
ROW = 4

LEVELS = (36, 40, 45)
CUTS = (6, 16, 27, 36, 43)
EVERY = 1

SMEM = pl.BlockSpec(memory_space=pltpu.SMEM)
VMEM = pl.BlockSpec(memory_space=pltpu.VMEM)
ANY = pl.BlockSpec(memory_space=pl.ANY)


def popcount(x):
    srl = lax.shift_right_logical
    x = x - (srl(x, jnp.int32(1)) & 0x55555555)
    x = (x & 0x33333333) + (srl(x, jnp.int32(2)) & 0x33333333)
    x = (x + srl(x, jnp.int32(4))) & 0x0F0F0F0F
    x = x + srl(x, jnp.int32(8))
    x = x + srl(x, jnp.int32(16))
    return x & 63


def list_kernel(n, nb, slots, tips, where, meta, zsend, xsend, codes, nums, live, union):
    srl = lax.shift_right_logical
    l, xcol = where[0], where[1]

    def fill(dev, _):
        total = jnp.int32(0)
        for b in range(nb):
            j = dev * nb + b
            start, count = meta[2 * j], meta[2 * j + 1]
            ones = (jnp.int32(1) << count) - 1
            bits = (ones << start) | srl(srl(ones, tips - 1 - start), jnp.int32(1))
            if tips < 32:
                bits = bits & ((1 << tips) - 1)
            live[j] = bits
            total = total | bits
        union[dev] = total
        return 0

    lax.fori_loop(0, n, fill, 0)

    def wrap(dev):
        return lax.rem(dev + n, n)

    def z_target(dev):
        base = (dev // ROW) * ROW
        at = dev - base
        total = union[wrap(base - 1)]
        for back in range(2, ROW + 1):
            got = union[wrap(base - back)]
            total = total | jnp.where(ROW - back >= at, got, 0)
        return total

    def x_target(dev):
        base = (dev // ROW) * ROW
        return union[base] | union[base + 1]

    def chip_counts(chip, most):
        zsum, xsum = jnp.int32(0), jnp.int32(0)
        for core in range(2):
            dev = 2 * chip + core
            zt, xt = z_target(dev), x_target(dev)
            for b in range(nb):
                bits = live[dev * nb + b]
                zsum = zsum + popcount(bits & zt)
                xsum = xsum + popcount(bits & xt)
        xsum = jnp.where(lax.rem(chip, 2) == 1, xsum, 0)
        return jnp.maximum(most, jnp.maximum(zsum, xsum))

    nums[4] = lax.fori_loop(0, n // 2, chip_counts, jnp.int32(0))

    own = union[l]

    def build(first, z, out, coded, base=0):
        def panel(jj, at):
            dev = first + jj // nb
            b = lax.rem(jj, nb)
            j = dev * nb + b
            target = jnp.where(z, z_target(dev), x_target(dev))
            need = live[j] & target
            start = meta[2 * j]
            shift = dev - l

            def slot(p, at):
                tip = start + p
                tip = jnp.where(tip >= tips, tip - tips, tip)
                if coded:
                    good = (shift >= 0) & (shift <= SHIFTS) & ((srl(own, tip) & 1) == 1)
                    out[at + base] = jnp.where(good, jj * tips + tip, -1)
                else:
                    out[at] = jj * slots + p
                return at + (srl(need, tip) & 1)

            return lax.fori_loop(0, meta[2 * j + 1], slot, at)

        return lax.fori_loop(0, 2 * nb, panel, jnp.int32(0))

    mine = 2 * xcol
    nums[0] = build(mine, True, zsend, False)
    nums[1] = build(mine, False, xsend, False)
    nums[2] = build(ROW + mine, True, codes, True)
    nums[3] = build(jnp.where(xcol == 0, 2, ROW), xcol == 1, codes, True, codes.shape[0] // 2)


def pack_kernel(pieces, nb, slots, where, zsend, xsend, nums, own, peer, *rest):
    outs, sems = rest[:-1], rest[-1]
    core = where[2]

    def issue(todo, listed, count, start, out, sem):
        def one(s, _):
            e = listed[2 * (s + start) + core]
            jj = e // slots
            p = lax.rem(e, slots)
            b = lax.rem(jj, nb)
            mine = (jj // nb) == core
            for source, yes in ((own, mine), (peer, jnp.logical_not(mine))):

                @pl.when(yes)
                def _():
                    copy = pltpu.make_async_copy(source.at[:, b, p], out.at[s], sem.at[s])
                    copy.start() if todo else copy.wait()

            return 0

        held = jnp.clip((count - core + 1) // 2 - start, 0, out.shape[0])
        lax.fori_loop(0, held, one, 0)

    for todo in (True, False):
        for i, ((is_x, start), out) in enumerate(zip(pieces, outs)):
            count = jnp.where(where[1] == 1, nums[1], 0) if is_x else nums[0]
            issue(todo, xsend if is_x else zsend, count, start, out, sems.at[i])


def product(left, tile):
    flat = tile.reshape(tile.shape[0] * tile.shape[1], tile.shape[2])
    return jnp.dot(left, flat, preferred_element_type=jnp.float32)


def add_to(acc, kb, got):
    nf, nb, _, rows, _ = acc.shape
    for a in range(nb):
        for h in range(nf):
            at = (a * nf + h) * rows
            acc[h, a, kb] += got[at : at + rows]


def run_list(count, group, entry, left, acc):
    def some(i, _):
        found = [entry(group * i + g) for g in range(group)]
        got = [product(left[t], tile) for t, tile, _ in found]
        for (_, _, kb), part in zip(found, got):
            add_to(acc, kb, part)
        return 0

    lax.fori_loop(0, (count + group - 1) // group, some, 0)


def own_kernel(nb, tips, meta, raw, resid, left, acc, grad):
    freqs, width = raw.shape[0], raw.shape[-1]
    acc[...] = jnp.zeros_like(acc)
    grad[...] = jnp.zeros_like(grad)

    def turn(t, _):
        for a in range(nb):
            start, count = meta[2 * a], meta[2 * a + 1]
            p = t - start
            p = jnp.where(p < 0, p + tips, p)

            @pl.when(p < count)
            def _():
                for f in range(freqs):
                    left[t, pl.ds(a * width, width), pl.ds(f * width, width)] = raw[f, a, p].T

            @pl.when(p >= count)
            def _():
                left[t, pl.ds(a * width, width), :] = jnp.zeros(
                    (width, freqs * width), left.dtype
                )

        return 0

    lax.fori_loop(0, tips, turn, 0)

    left[tips] = jnp.zeros(left.shape[1:], left.dtype)
    for b in range(nb):
        start, count = meta[2 * b], meta[2 * b + 1]

        def one(i, _):
            for g in range(GROUP):
                p = GROUP * i + g
                t = start + p
                t = jnp.where(t >= tips, t - tips, t)
                t = jnp.where(p < count, t, tips)
                tile = raw[:, b, jnp.minimum(p, count - 1)]
                add_to(acc, b, product(left[t], tile))
                grad[b] += product(resid[t], tile)
            return 0

        lax.fori_loop(0, (count + GROUP - 1) // GROUP, one, 0)


def peer_kernel(tips, where, meta, left, raw, acc):
    acc[...] = jnp.zeros_like(acc)

    @pl.when(where[2] == 0)
    def _():
        nb = raw.shape[1]

        def panel(b, _):
            start, count = meta[2 * (nb + b)], meta[2 * (nb + b) + 1]

            def entry(p):
                t = start + p
                t = jnp.where(t >= tips, t - tips, t)
                t = jnp.where(p < count, t, tips)
                return t, raw[:, b, jnp.minimum(p, count - 1)], b

            run_list(count, GROUP, entry, left, acc)
            return 0

        lax.fori_loop(0, nb, panel, 0)


def chunk_kernel(tips, spans, first, where, codes, nums, left, *rest):
    held_in = rest[0] if not first else None
    arrays = rest[(0 if first else 1) : -3]
    acc, tiles, sems = rest[-3:]
    core = where[2]
    copies = []
    place = 0
    places = []
    for i, array in enumerate(arrays):
        size = array.shape[0]
        copies.append(pltpu.make_async_copy(array, tiles.at[pl.ds(place, size)], sems.at[i]))
        places.append((place, size))
        place += size
    for copy in copies:
        copy.start()
    if first:
        acc[...] = jnp.zeros_like(acc)
    else:
        acc[...] = held_in[...]
    for copy in copies:
        copy.wait()
    columns = acc.shape[2] // 2

    def array(q, _):
        def pick(values):
            got = jnp.int32(values[0])
            for i, v in enumerate(values[1:], 1):
                got = jnp.where(q == i, v, got)
            return got

        is_b = pick([int(b) for b, _, _ in spans])
        other = pick([int(o) for _, o, _ in spans])
        offset = pick([o for _, _, o in spans])
        place = pick([p for p, _ in places])
        size = pick([z for _, z in places])
        holder = jnp.where(other == 1, 1 - core, core)
        count = jnp.where(is_b == 1, nums[3], nums[2])
        held = jnp.clip((count - holder + 1) // 2 - offset, 0, size)
        base = is_b * (codes.shape[0] // 2) + 2 * offset + holder

        def entry(s):
            at = jnp.minimum(s, held - 1)
            code = codes[2 * at + base]
            good = (code >= 0) & (s < held)
            t = jnp.where(good, lax.rem(code, tips), tips)
            column = jnp.where(good, code // tips, columns - 1) + is_b * columns
            return t, tiles[place + at], column

        run_list(held, GROUP, entry, left, acc)
        return 0

    lax.fori_loop(0, len(spans), array, 0)


def add_kernel(*refs):
    total = refs[0][...]
    for ref in refs[1:-1]:
        total = total + ref[...]
    refs[-1][...] = total


def call(kernel, outs, specs, out_specs, scratch=(), cost_us=0):
    return pl.pallas_call(
        kernel,
        out_shape=outs,
        in_specs=specs,
        out_specs=out_specs,
        scratch_shapes=scratch,
        cost_estimate=pl.CostEstimate(
            flops=int(cost_us * 1e9), transcendentals=0, bytes_accessed=int(cost_us * 1e6)
        ),
        compiler_params=pltpu.CompilerParams(vmem_limit_bytes=16000 * 1024),
    )


def on_device(tiles, tip_lists, counts, residual):
    freqs, nb, slots, width = tiles.shape[:4]
    tips = residual.shape[1] // width
    n = lax.axis_size("cells")
    nf = lax.axis_size("freq")
    rows = width // nf
    d = lax.axis_index("cells").astype(jnp.int32)
    fi = lax.axis_index("freq")
    i32 = jnp.int32

    def moved(x, to):
        return lax.ppermute(x, "cells", [(i, to(i) % n) for i in range(n)])

    own_meta = jnp.stack([tip_lists[:, 0], counts], axis=1).reshape(-1).astype(i32)
    meta = own_meta
    have = 1
    peer = None
    while have < n:
        steps = [k for k in range(1, ROW) if k * have < n]
        got = [moved(meta, lambda i, k=k: i - k * have) for k in steps]
        if have == 1:
            *got, hold = lax.optimization_barrier((*got, tiles))
            peer = moved(hold, lambda i: i ^ 1)
        meta = jnp.concatenate(
            [meta] + [x[: min(have, n - k * have) * 2 * nb] for k, x in zip(steps, got)]
        )
        have = meta.shape[0] // (2 * nb)
    l = lax.rem(d, i32(ROW))
    xcol = lax.rem(d // 2, i32(2))
    core = lax.rem(d, i32(2))
    where = jnp.stack([l, xcol, core])
    per = 2 * nb
    row_meta = lax.dynamic_slice(
        jnp.concatenate([meta, meta]), (lax.rem(n - l, i32(n)) * per,), (n * per,)
    )

    ints = lambda m: jax.ShapeDtypeStruct((m,), i32)
    room = 2 * nb * slots + 8
    zsend, xsend, codes, nums = call(
        functools.partial(list_kernel, n, nb, slots, tips),
        (ints(room), ints(room), ints(2 * room), ints(8)),
        [SMEM] * 2,
        (SMEM,) * 4,
        [pltpu.SMEM((n * nb,), i32), pltpu.SMEM((n,), i32)],
        cost_us=6,
    )(where, row_meta)

    resid = residual.reshape(freqs, tips, width).transpose(1, 0, 2).reshape(tips, 1, freqs * width)
    resid = jnp.pad(
        jnp.broadcast_to(resid, (tips, 16, freqs * width)), ((0, 1), (0, 0), (0, 0))
    )

    def sums(columns):
        return jax.ShapeDtypeStruct((nf, nb, columns, rows, width), jnp.float32)

    def joined(x):
        got = lax.dynamic_index_in_dim(x, fi, 0, keepdims=False)
        for s in range(1, nf):
            part = lax.dynamic_index_in_dim(x, lax.rem(fi + s, nf), 0, keepdims=False)
            pairs = [(i, (i + s) % nf) for i in range(nf)]
            got = got + lax.ppermute(part, "freq", pairs)
        return got

    def pack(pieces):
        shapes = tuple(
            jax.ShapeDtypeStruct((end - at, freqs, width, width), tiles.dtype)
            for _, at, end in pieces
        )
        return call(
            functools.partial(pack_kernel, [p[:2] for p in pieces], nb, slots),
            shapes,
            [SMEM] * 4 + [ANY] * 2,
            (VMEM,) * len(shapes),
            [pltpu.SemaphoreType.DMA((len(shapes), max(x.shape[0] for x in shapes)))],
            cost_us=6,
        )(where, zsend, xsend, nums, tiles, peer)

    def chunk(pieces, total):
        spans = [s for s, _ in pieces]
        arrays = [x for _, x in pieces]
        first = total is None
        specs = [SMEM] * 3 + [VMEM] * (1 if first else 2) + [ANY] * len(arrays)
        scratch = [
            pltpu.VMEM((sum(x.shape[0] for x in arrays), freqs, width, width), tiles.dtype),
            pltpu.SemaphoreType.DMA((len(arrays),)),
        ]
        more = () if first else (total,)
        return lambda left: call(
            functools.partial(chunk_kernel, tips, spans, first),
            sums(2 * (2 * nb + 1)),
            specs,
            VMEM,
            scratch,
            cost_us=14,
        )(where, codes, nums, left, *more, *arrays)

    def main(cuts):
        return parts(cuts)

    def parts(cuts):
        spots = list(zip((0,) + cuts, cuts))
        zpack = list(pack([(False,) + spots[0]]))
        rest = [(False,) + s for s in spots[1:]] + [(True,) + s for s in spots]
        later = pack(rest)
        zpack += later[: len(spots) - 1]
        xpack = later[len(spots) - 1 :]
        landed = [moved(z, lambda i: i - ROW) for z in zpack]
        left, own, grad = call(
            functools.partial(own_kernel, nb, tips),
            (
                jax.ShapeDtypeStruct((tips + 1, nb * width, freqs * width), tiles.dtype),
                sums(nb),
                jax.ShapeDtypeStruct((nb, 16, width), jnp.float32),
            ),
            [SMEM, VMEM, VMEM],
            (VMEM, VMEM, VMEM),
            cost_us=25,
        )(own_meta, tiles, resid)
        gate = own
        total = None
        ready = []
        peers = None
        for i, (at, end) in enumerate(spots):
            a = landed[i]
            if i > 1:
                a, gate = lax.optimization_barrier((a, gate))
            b = moved(jnp.where(xcol == 0, a, xpack[i]), lambda i: i ^ 2)
            a_peer = moved(a, lambda i: i ^ 1)
            ready += [((False, False, at), a), ((False, True, at), a_peer)]
            if i == 0:
                peers = gate = call(
                    functools.partial(peer_kernel, tips),
                    sums(nb),
                    [SMEM, SMEM, VMEM, VMEM],
                    VMEM,
                    cost_us=12,
                )(where, meta, left, peer)
                early = joined(jnp.concatenate([own, peers], axis=2))
                grad = grad[:, 0, :]
                grads = [grad]
                for s in range(1, nf):
                    pairs = [(i, (i + s) % nf) for i in range(nf)]
                    grads.append(lax.ppermute(grad, "freq", pairs))
                grad_sum = call(
                    add_kernel,
                    jax.ShapeDtypeStruct(grad.shape, grad.dtype),
                    [VMEM] * nf,
                    VMEM,
                    cost_us=1,
                )(*grads)
            elif (len(spots) - 1 - i) % EVERY == 0:
                gate = total = chunk(ready, total)(left)
                ready = []
            b, gate = lax.optimization_barrier((b, gate))
            b_peer = moved(b, lambda i: i ^ 1)
            ready += [((True, False, at), b), ((True, True, at), b_peer)]
        firsts = joined(total[:, :, : 2 * nb])
        total = chunk(ready, total)(left)
        seconds = joined(total[:, :, 2 * nb + 1 : 4 * nb + 1])
        all_of = jnp.concatenate([early, seconds, firsts], axis=1)
        own_part, rest = all_of[:, :nb], all_of[:, nb:]
        columns = SHIFTS * nb
        rest = jnp.where(core == 0, rest[:, :columns], rest[:, nb : nb + columns])
        band = jnp.concatenate([own_part, rest], axis=1)
        return band, grad_sum

    full = nb * slots
    levels = [full * m // 60 for m in LEVELS] + [full]
    need = (nums[4] + 1) // 2
    level = sum((need > h).astype(i32) for h in levels[:-1])

    def cuts_of(half):
        return tuple(half * m // CUTS[-1] for m in CUTS)

    band, grad = lax.switch(level, [functools.partial(main, cuts_of(h)) for h in levels])
    return (
        band.reshape(nb, SHIFTS + 1, nb, rows, width),
        grad.reshape(nb * width),
    )


def solution(mesh):
    placed = (P("freq", "cells", None, None, None), P("cells", None), P("cells"), P("freq", None))
    return jax.shard_map(
        on_device,
        mesh=mesh,
        in_specs=placed,
        out_specs=(P("cells", None, None, "freq", None), P("cells")),
        check_vma=False,
    )
```
